32 devices in a mesh: days: 2 (over x), tm: 8 (over z, y), sta: 2 (over core).
Axes of the slice: x: 2, y: 2, z: 4, core: 2. Of those that a mesh axis runs over, the one named last changes fastest.
Arguments:
- records: bfloat16 [2048, 2048], P('sta', ('days', 'tm')), parts along dimension 1, may hold values from -6 to 6
- following: bfloat16 [2048, 510], P('sta', 'days'), parts along dimension 1, may hold values from -6 to 6
- library: bfloat16 [32, 2048, 256], P(None, ('sta', 'tm')), may hold values from -6 to 6
- template_ids: int32 [2, 8], replicated, may hold values from 0 to 31
- channel_mask: int32 [32, 2048], replicated, may hold values 0 or 1
- station_group: int32 [2048], replicated, may hold values from 0 to 127
Outputs:
- detection: float32 [2, 8, 2048], P('sta', None, ('days', 'tm')), parts along dimension 2
The draws below stay inside these ranges and needn't reach their ends.
There are 2 independent parts, one for each index of `days`. The reference program is written for one: setup_inputs(seed, part) draws one part's arguments, and reference() takes and returns one part's arrays. A program takes and returns all parts, laid end to end along the dimension named above; an argument that names none is the same for every part. Nothing has to cross between parts.
All inputs are finite; a program needn't handle non-finite values.
Results may differ from the reference program's by a relative error of at most 0.0003.
Values may be sent and summed in bfloat16 or wider, within the bound.
A program may use at most 128 MiB of HBM per device.

```python
import math
import jax
import jax.numpy as jnp
import numpy as np
from jax import lax

S = 2048
W = 256
NLIB = 32
NB = 2
KB = 8
G = 128
T_SIZE = 1024


def touch_ends(values, key, low, largest):
    longest = values.shape.index(max(values.shape))
    spots = []
    for shift in (0, 1):
        where = [jax.random.randint(jax.random.fold_in(key, axis), (), 0, length) for axis, length in enumerate(values.shape)]
        where[longest] = (where[longest] + shift) % values.shape[longest]
        spots.append(tuple(where))
    return values.at[spots[0]].set(low).at[spots[1]].set(largest)


def shard_levels(own_key, shape, pieces, least, largest):
    gain, own = 1.0, jax.random.fold_in(own_key, 6)
    for axis_at, blocks in pieces:
        steps = jnp.exp(jax.random.uniform(jax.random.fold_in(own, axis_at), (blocks,), jnp.float32, least / len(pieces), largest / len(pieces)))
        gain = gain * jnp.repeat(steps, shape[axis_at] // blocks).reshape([-1 if axis == axis_at else 1 for axis in range(len(shape))])
    return gain


def rank_bounds(number_of, skew):
    portions = [(1 << 20) // math.isqrt(grade ** skew) + 1 for grade in range(1, number_of + 1)]
    spread = 1 + sum(portions) // (1 << 30)
    return np.cumsum(np.array([max(1, weight // spread) for weight in portions]))


def skewed_ids(own_key, extent, number_of, lean):
    table = rank_bounds(number_of, lean)
    lot = jax.random.randint(jax.random.fold_in(own_key, 1), extent, 0, int(table[number_of - 1]))
    standing = jnp.searchsorted(jnp.asarray(table, jnp.int32), lot, side="right")
    return jax.random.permutation(jax.random.fold_in(own_key, 2), number_of)[standing].astype(jnp.int32)


def scatter_about(key, extent, spread, reach, split=(), kind=jnp.bfloat16):
    array = spread * jax.random.normal(key, extent, jnp.float32)
    if split:
        array = array * shard_levels(key, extent, split, -0.22, 0.18)
    return jnp.clip(array, -reach, reach).astype(kind)


def setup_inputs(seed: int = 0, part: int = 0) -> dict:
    key_of = jax.random.split(jax.random.key(seed), 7)
    part_splits = jax.random.split(jax.random.fold_in(key_of[6], part), 7)
    return {
        "records": scatter_about(part_splits[0], (S, T_SIZE), 1.0, 6.0, ((0, 2), (1, 8))),
        "following": scatter_about(part_splits[1], (S, W - 1), 1.0, 6.0, ((0, 2),)),
        "library": scatter_about(key_of[2], (NLIB, S, W), 1.0, 6.0, ((1, 16),)),
        "template_ids": touch_ends(jax.random.randint(key_of[3], (NB, KB), 0, NLIB), jax.random.fold_in(key_of[3], 1), 0, NLIB - 1).astype(jnp.int32),
        "channel_mask": touch_ends((jax.random.randint(key_of[4], (NLIB, S), 0, 2) < 1).astype(jnp.int32), jax.random.fold_in(key_of[4], 1), 0, 1),
        "station_group": touch_ends(skewed_ids(key_of[5], (S,), G, 2), jax.random.fold_in(key_of[5], 3), 0, G - 1).astype(jnp.int32),
    }


epsilon = 1e-06

def reference(records, following, library, template_ids, channel_mask, station_group):
    stream = jnp.concatenate([records, following], axis=1)
    squares = stream.astype(jnp.float32) ** 2
    energy = lax.reduce_window(squares, jnp.float32(0), lax.add, (1, W), (1, 1), 'VALID') / W
    inverse = 1.0 / jnp.sqrt(energy + epsilon)
    onehot = (station_group[:, None] == jnp.arange(G, dtype=jnp.int32)[None, :]).astype(jnp.int32)
    counts = jnp.dot(channel_mask, onehot, preferred_element_type=jnp.int32)
    per_station = jnp.take(counts, station_group, axis=1)
    tmean = lax.optimization_barrier(jnp.mean(library.astype(jnp.float32) ** 2, axis=2))
    coef = channel_mask.astype(jnp.float32) / jnp.sqrt(jnp.float32(W * G) * jnp.maximum(per_station, 1).astype(jnp.float32) * (tmean + epsilon))
    flat_ids = template_ids.reshape(-1)
    chosen = jnp.take(library, flat_ids, axis=0)
    weights = jnp.take(coef, flat_ids, axis=0)
    block_size = math.gcd(S, 16)
    grid = jnp.arange(W, dtype=jnp.int32)[:, None] + jnp.arange(T_SIZE, dtype=jnp.int32)[None, :]

    def advance(running, index):
        first = (index * block_size).astype(jnp.int32)
        rows = lax.dynamic_slice_in_dim(stream, first, block_size, 0)
        hankel = rows[:, grid].astype(jnp.float32)
        temps = lax.dynamic_slice_in_dim(chosen, first, block_size, 1).astype(jnp.float32)
        corr = jnp.einsum('jbw,bwt->jbt', temps, hankel)
        weight = lax.dynamic_slice_in_dim(weights, first, block_size, 1)
        scale = lax.dynamic_slice_in_dim(inverse, first, block_size, 0)
        return (running + lax.optimization_barrier(jnp.sum(corr * weight[:, :, None] * scale[None], axis=1)), None)
    start_zero = jnp.zeros((NB * KB, T_SIZE), jnp.float32)
    result = lax.scan(advance, start_zero, jnp.arange(S // block_size, dtype=jnp.int32))[0]
    return result.reshape(NB, KB, T_SIZE)
```

```python
import functools

import jax
import jax.numpy as jnp
from jax import lax
from jax.experimental import pallas as pl
from jax.experimental.pallas import tpu as pltpu
from jax.sharding import PartitionSpec as P

G = 128
LANES = 128
ROWS = 16


epsilon = 1e-06


def correlate_group(chunk, window, stream_ref, temps_ref, weights_ref, out_ref, base, hankel, scale):
    length = chunk + window
    group = stream_ref.shape[0]
    start = pl.multiple_of(pl.program_id(0) * chunk, LANES)
    rows = stream_ref[:, pl.ds(start, length)]

    total = rows * rows
    span = 1
    while span < LANES:
        total = total + pltpu.roll(total, length - span, 1)
        span *= 2
    energy = total[:, :chunk]
    for step in range(1, window // LANES):
        energy = energy + total[:, step * LANES : step * LANES + chunk]
    scale[...] = lax.rsqrt(energy / window + epsilon)

    for shift in range(ROWS):
        moved = rows if shift == 0 else pltpu.roll(rows, length - shift, 1)
        for block in range(length // LANES):
            base[block, pl.ds(shift, group, stride=ROWS), :] = moved[:, block * LANES : (block + 1) * LANES]

    wide = length - LANES
    acc = None
    for s in range(group):
        slot = s % hankel.shape[0]
        shifted = jnp.concatenate(
            [base[block, s * ROWS : (s + 1) * ROWS, :] for block in range(length // LANES)], axis=1
        ).astype(jnp.bfloat16)
        for part in range(LANES // ROWS):
            hankel[slot, part * ROWS : (part + 1) * ROWS, :] = shifted[:, part * ROWS : part * ROWS + wide]
        matrix = jnp.concatenate(
            [hankel[slot, :, step * LANES : step * LANES + chunk] for step in range(window // LANES)], axis=0
        )
        corr = jnp.dot(temps_ref[s], matrix, preferred_element_type=jnp.float32)
        term = corr * scale[s : s + 1, :] * weights_ref[0, :, s : s + 1]
        acc = term if acc is None else acc + term

    @pl.when(pl.program_id(1) == 0)
    def _():
        out_ref[...] = acc

    @pl.when(pl.program_id(1) != 0)
    def _():
        out_ref[...] += acc


def station_sums(stream, temps, weights, out_len):
    stations, slots, window = temps.shape
    group = min(16, stations)
    chunk = min(1024, out_len)
    length = chunk + window
    full = stream.shape[1]
    groups = stations // group
    weights = jnp.transpose(weights.reshape(slots, groups, group), (1, 0, 2))
    return pl.pallas_call(
        functools.partial(correlate_group, chunk, window),
        grid=(out_len // chunk, groups),
        in_specs=[
            pl.BlockSpec((group, full), lambda c, g: (g, 0)),
            pl.BlockSpec((group, slots, window), lambda c, g: (g, 0, 0)),
            pl.BlockSpec((1, slots, group), lambda c, g: (g, 0, 0)),
        ],
        out_specs=pl.BlockSpec((slots, chunk), lambda c, g: (0, c)),
        out_shape=jax.ShapeDtypeStruct((slots, out_len), jnp.float32),
        scratch_shapes=[
            pltpu.VMEM((length // LANES, group * ROWS, LANES), jnp.float32),
            pltpu.VMEM((2, LANES, length - LANES), jnp.bfloat16),
            pltpu.VMEM((group, chunk), jnp.float32),
        ],
        name="station_sums",
    )(stream, temps, weights)


def station_weights(channel_mask, station_group, flat_ids, chosen, first, sub_rows):
    window = chosen.shape[2]
    mask = jnp.take(channel_mask, flat_ids, axis=0)
    mine = lax.dynamic_slice_in_dim(station_group, first, sub_rows, 0)
    same = (station_group[:, None] == mine[None, :]).astype(jnp.bfloat16)
    counts = jnp.dot(mask.astype(jnp.bfloat16), same, preferred_element_type=jnp.float32)
    my_mask = lax.dynamic_slice_in_dim(mask, first, sub_rows, 1).astype(jnp.float32)
    tmean = jnp.mean(jnp.square(chosen.astype(jnp.float32)), axis=2)
    return my_mask / jnp.sqrt(jnp.float32(window * G) * jnp.maximum(counts, 1.0) * (tmean + epsilon))


def shards(records, following, library, template_ids, channel_mask, station_group):
    sta_rows, block_len = records.shape
    sub_rows = library.shape[1]
    batches, per_batch = template_ids.shape
    flat_ids = template_ids.reshape(-1)
    offset = lax.axis_index("tm") * sub_rows
    first = lax.axis_index("sta") * sta_rows + offset
    moved = lax.all_to_all(records, "tm", split_axis=0, concat_axis=1, tiled=True)
    chosen = jnp.take(library, flat_ids, axis=0)
    weights = station_weights(channel_mask, station_group, flat_ids, chosen, first, sub_rows)
    temps = jnp.transpose(chosen, (1, 0, 2))
    tail_rows = lax.dynamic_slice_in_dim(following, offset, sub_rows, 0)
    pad = jnp.zeros((sub_rows, library.shape[2] - tail_rows.shape[1]), records.dtype)
    stream = jnp.concatenate([moved, tail_rows, pad], axis=1).astype(jnp.float32)
    partial_sum = station_sums(stream, temps, weights, moved.shape[1])
    totals = lax.psum_scatter(partial_sum, "tm", scatter_dimension=1, tiled=True)
    return lax.psum_scatter(
        totals.reshape(batches, per_batch, block_len), "sta", scatter_dimension=0, tiled=True
    )


def solution(mesh):
    placed = (
        P("sta", ("days", "tm")),
        P("sta", "days"),
        P(None, ("sta", "tm"), None),
        P(),
        P(),
        P(),
    )
    return jax.shard_map(
        shards,
        mesh=mesh,
        in_specs=placed,
        out_specs=P("sta", None, ("days", "tm")),
        check_vma=False,
    )
```

```python
import functools

import jax
import jax.numpy as jnp
from jax import lax
from jax.experimental import pallas as pl
from jax.experimental.pallas import tpu as pltpu
from jax.sharding import PartitionSpec as P

G = 128
LANES = 128
ROWS = 16


epsilon = 1e-06


def correlate_group(chunk, window, stream_ref, temps_ref, weights_ref, out_ref, base, hankel, scale):
    length = chunk + window
    group = stream_ref.shape[0]
    start = pl.multiple_of(pl.program_id(0) * chunk, LANES)
    rows = stream_ref[:, pl.ds(start, length)]

    total = rows * rows
    span = 1
    while span < LANES:
        total = total + pltpu.roll(total, length - span, 1)
        span *= 2
    energy = total[:, :chunk]
    for step in range(1, window // LANES):
        energy = energy + total[:, step * LANES : step * LANES + chunk]
    scale[...] = lax.rsqrt(energy / window + epsilon)

    for shift in range(ROWS):
        moved = rows if shift == 0 else pltpu.roll(rows, length - shift, 1)
        for block in range(length // LANES):
            base[block, pl.ds(shift, group, stride=ROWS), :] = moved[:, block * LANES : (block + 1) * LANES]

    wide = length - LANES
    acc = None
    for s in range(group):
        slot = s % hankel.shape[0]
        shifted = jnp.concatenate(
            [base[block, s * ROWS : (s + 1) * ROWS, :] for block in range(length // LANES)], axis=1
        ).astype(jnp.bfloat16)
        for part in range(LANES // ROWS):
            hankel[slot, part * ROWS : (part + 1) * ROWS, :] = shifted[:, part * ROWS : part * ROWS + wide]
        matrix = jnp.concatenate(
            [hankel[slot, :, step * LANES : step * LANES + chunk] for step in range(window // LANES)], axis=0
        )
        corr = jnp.dot(temps_ref[s], matrix, preferred_element_type=jnp.float32)
        term = corr * scale[s : s + 1, :] * weights_ref[0, :, s : s + 1]
        acc = term if acc is None else acc + term

    parts = [acc[:, block * LANES : (block + 1) * LANES] for block in range(chunk // LANES)]

    @pl.when(pl.program_id(1) == 0)
    def _():
        for block, part in enumerate(parts):
            out_ref[block] = part

    @pl.when(pl.program_id(1) != 0)
    def _():
        for block, part in enumerate(parts):
            out_ref[block] += part


def station_sums(stream, temps, weights, out_len):
    stations, slots, window = temps.shape
    group = min(16, stations)
    chunk = min(1024, out_len)
    length = chunk + window
    full = stream.shape[1]
    groups = stations // group
    weights = jnp.transpose(weights.reshape(slots, groups, group), (1, 0, 2))
    return pl.pallas_call(
        functools.partial(correlate_group, chunk, window),
        grid=(out_len // chunk, groups),
        in_specs=[
            pl.BlockSpec((group, full), lambda c, g: (g, 0)),
            pl.BlockSpec((group, slots, window), lambda c, g: (g, 0, 0)),
            pl.BlockSpec((1, slots, group), lambda c, g: (g, 0, 0)),
        ],
        out_specs=pl.BlockSpec((chunk // LANES, slots, LANES), lambda c, g: (c, 0, 0)),
        out_shape=jax.ShapeDtypeStruct((out_len // LANES, slots, LANES), jnp.float32),
        scratch_shapes=[
            pltpu.VMEM((length // LANES, group * ROWS, LANES), jnp.float32),
            pltpu.VMEM((2, LANES, length - LANES), jnp.bfloat16),
            pltpu.VMEM((group, chunk), jnp.float32),
        ],
        name="station_sums",
    )(stream, temps, weights)


def enter(peers):
    barrier = pltpu.get_barrier_semaphore()
    for peer in peers:
        pl.semaphore_signal(barrier, inc=1, device_id=peer, device_id_type=pl.DeviceIdType.MESH)
    pl.semaphore_wait(barrier, len(peers))


def collect_rows(count, records_ref, following_ref, stream_ref, held, tail, own_sem, send_sem, recv_sem):
    me = lax.axis_index("tm")
    rows, block_len = held.shape[1:]
    offset = pl.multiple_of(me * rows, rows)
    own = pltpu.make_async_copy(records_ref.at[pl.ds(offset, rows), :], held.at[me], own_sem.at[0])
    after = pltpu.make_async_copy(following_ref.at[pl.ds(offset, rows), :], tail, own_sem.at[1])
    own.start()
    after.start()
    others = [lax.rem(me + step, count) for step in range(1, count)]
    enter([{"tm": other} for other in others])
    copies = []
    for step, other in enumerate(others):
        copy = pltpu.make_async_remote_copy(
            src_ref=records_ref.at[pl.ds(pl.multiple_of(other * rows, rows), rows), :],
            dst_ref=held.at[me],
            send_sem=send_sem.at[step],
            recv_sem=recv_sem.at[step],
            device_id={"tm": other},
            device_id_type=pl.DeviceIdType.MESH,
        )
        copy.start()
        copies.append(copy)
    after.wait()
    out_len = count * block_len
    stream_ref[:, out_len:] = jnp.zeros((rows, stream_ref.shape[1] - out_len), jnp.float32)
    stream_ref[:, out_len : out_len + tail.shape[1]] = tail[...].astype(jnp.float32)
    own.wait()
    for copy in copies:
        copy.wait()
    for block in range(count):
        stream_ref[:, block * block_len : (block + 1) * block_len] = held[block].astype(jnp.float32)


def collect_stream(records, following, count, window):
    sta_rows, block_len = records.shape
    rows = sta_rows // count
    return pl.pallas_call(
        functools.partial(collect_rows, count),
        in_specs=[pl.BlockSpec(memory_space=pl.ANY)] * 2,
        out_specs=pl.BlockSpec(memory_space=pltpu.VMEM),
        out_shape=jax.ShapeDtypeStruct((rows, count * block_len + window), jnp.float32),
        scratch_shapes=[
            pltpu.VMEM((count, rows, block_len), records.dtype),
            pltpu.VMEM((rows, following.shape[1]), following.dtype),
            pltpu.SemaphoreType.DMA((2,)),
            pltpu.SemaphoreType.DMA((count - 1,)),
            pltpu.SemaphoreType.DMA((count - 1,)),
        ],
        compiler_params=pltpu.CompilerParams(collective_id=0, has_side_effects=True),
        name="collect_stream",
    )(records, following)


def reduce_blocks(parts_ref, out_ref, held, send_sem, recv_sem):
    blocks, halves = parts_ref.shape[0], parts_ref.shape[1]
    count = blocks * halves
    block, half = lax.axis_index("tm"), lax.axis_index("sta")
    me = block * halves + half
    others = []
    for step in range(1, count):
        other = lax.rem(me + step, count)
        others.append((other // halves, lax.rem(other, halves)))
    enter([{"tm": b, "sta": h} for b, h in others])
    copies = []
    for step, (b, h) in enumerate(others):
        copy = pltpu.make_async_remote_copy(
            src_ref=parts_ref.at[b, h],
            dst_ref=held.at[step],
            send_sem=send_sem.at[step],
            recv_sem=recv_sem.at[step],
            device_id={"tm": b, "sta": h},
            device_id_type=pl.DeviceIdType.MESH,
        )
        copy.start()
        copies.append(copy)
    total = parts_ref[block, half]
    for step, copy in enumerate(copies):
        copy.wait_recv()
        total = total + held[step]
    out_ref[...] = total
    for copy in copies:
        copy.wait_send()


def reduce_parts(parts):
    count = parts.shape[0] * parts.shape[1]
    return pl.pallas_call(
        reduce_blocks,
        in_specs=[pl.BlockSpec(memory_space=pltpu.VMEM)],
        out_specs=pl.BlockSpec(memory_space=pltpu.VMEM),
        out_shape=jax.ShapeDtypeStruct(parts.shape[2:], parts.dtype),
        scratch_shapes=[
            pltpu.VMEM((count - 1,) + parts.shape[2:], parts.dtype),
            pltpu.SemaphoreType.DMA((count - 1,)),
            pltpu.SemaphoreType.DMA((count - 1,)),
        ],
        compiler_params=pltpu.CompilerParams(collective_id=1, has_side_effects=True),
        name="reduce_parts",
    )(parts)


def station_weights(channel_mask, station_group, flat_ids, chosen, first, sub_rows):
    window = chosen.shape[2]
    mask = jnp.take(channel_mask, flat_ids, axis=0)
    mine = lax.dynamic_slice_in_dim(station_group, first, sub_rows, 0)
    same = (station_group[:, None] == mine[None, :]).astype(jnp.bfloat16)
    counts = jnp.dot(mask.astype(jnp.bfloat16), same, preferred_element_type=jnp.float32)
    my_mask = lax.dynamic_slice_in_dim(mask, first, sub_rows, 1).astype(jnp.float32)
    tmean = jnp.mean(jnp.square(chosen.astype(jnp.float32)), axis=2)
    return my_mask / jnp.sqrt(jnp.float32(window * G) * jnp.maximum(counts, 1.0) * (tmean + epsilon))


def shards(blocks, halves, records, following, library, template_ids, channel_mask, station_group):
    sta_rows, block_len = records.shape
    sub_rows, window = library.shape[1:]
    batches, per_batch = template_ids.shape
    flat_ids = template_ids.reshape(-1)
    first = lax.axis_index("sta") * sta_rows + lax.axis_index("tm") * sub_rows
    stream = collect_stream(records, following, blocks, window)
    chosen = jnp.take(library, flat_ids, axis=0)
    weights = station_weights(channel_mask, station_group, flat_ids, chosen, first, sub_rows)
    temps = jnp.transpose(chosen, (1, 0, 2))
    sums = station_sums(stream, temps, weights, blocks * block_len)
    tiles = block_len // LANES
    parts = sums.reshape(blocks, tiles, halves, batches // halves * per_batch, LANES)
    parts = jnp.swapaxes(parts, 1, 2).reshape(blocks, halves, -1, LANES)
    mine = reduce_parts(parts).reshape(tiles, batches // halves, per_batch, LANES)
    return jnp.moveaxis(mine, 0, 2).reshape(batches // halves, per_batch, block_len)


def solution(mesh):
    placed = (
        P("sta", ("days", "tm")),
        P("sta", "days"),
        P(None, ("sta", "tm"), None),
        P(),
        P(),
        P(),
    )
    return jax.shard_map(
        functools.partial(shards, mesh.shape["tm"], mesh.shape["sta"]),
        mesh=mesh,
        in_specs=placed,
        out_specs=P("sta", None, ("days", "tm")),
        check_vma=False,
    )
```

```python
import functools

import jax
import jax.numpy as jnp
from jax import lax
from jax.experimental import pallas as pl
from jax.experimental.pallas import tpu as pltpu
from jax.sharding import PartitionSpec as P

G = 128
LANES = 128
ROWS = 16


epsilon = 1e-06


def correlate_group(chunk, window, stream_ref, temps_ref, weights_ref, out_ref, base, hankel, scale):
    length = chunk + window
    group = stream_ref.shape[0]
    start = pl.multiple_of(pl.program_id(0) * chunk, LANES)
    rows = stream_ref[:, pl.ds(start, length)]

    total = rows * rows
    span = 1
    while span < LANES:
        total = total + pltpu.roll(total, length - span, 1)
        span *= 2
    energy = total[:, :chunk]
    for step in range(1, window // LANES):
        energy = energy + total[:, step * LANES : step * LANES + chunk]
    scale[...] = lax.rsqrt(energy / window + epsilon)

    for shift in range(ROWS):
        moved = rows if shift == 0 else pltpu.roll(rows, length - shift, 1)
        for block in range(length // LANES):
            base[block, pl.ds(shift, group, stride=ROWS), :] = moved[:, block * LANES : (block + 1) * LANES]

    wide = length - LANES
    slots, lanes = weights_ref.shape
    turn = lax.rem(lanes - pl.program_id(1) * group, lanes)
    weights = pltpu.roll(weights_ref[...], turn, 1)
    acc = None
    for s in range(group):
        template = [temps_ref[block, s * slots : (s + 1) * slots, :] for block in range(window // LANES)]
        squares = sum(piece * piece for piece in template)
        tmean = jnp.sum(squares, axis=1, keepdims=True) / window
        weight = weights[:, s : s + 1] * lax.rsqrt(tmean + epsilon)
        template = jnp.concatenate(template, axis=1).astype(jnp.bfloat16)
        slot = s % hankel.shape[0]
        shifted = jnp.concatenate(
            [base[block, s * ROWS : (s + 1) * ROWS, :] for block in range(length // LANES)], axis=1
        ).astype(jnp.bfloat16)
        for part in range(LANES // ROWS):
            hankel[slot, part * ROWS : (part + 1) * ROWS, :] = shifted[:, part * ROWS : part * ROWS + wide]
        matrix = jnp.concatenate(
            [hankel[slot, :, step * LANES : step * LANES + chunk] for step in range(window // LANES)], axis=0
        )
        corr = jnp.dot(template, matrix, preferred_element_type=jnp.float32)
        term = corr * scale[s : s + 1, :] * weight
        acc = term if acc is None else acc + term

    parts = [acc[:, block * LANES : (block + 1) * LANES] for block in range(chunk // LANES)]

    @pl.when(pl.program_id(1) == 0)
    def _():
        for block, part in enumerate(parts):
            out_ref[block] = part

    @pl.when(pl.program_id(1) != 0)
    def _():
        for block, part in enumerate(parts):
            out_ref[block] += part


def station_sums(stream, temps, weights, out_len):
    stations = stream.shape[0]
    slots, lanes = weights.shape
    window = temps.shape[0] * LANES
    group = min(16, stations)
    chunk = min(1024, out_len)
    length = chunk + window
    full = stream.shape[1]
    groups = stations // group
    return pl.pallas_call(
        functools.partial(correlate_group, chunk, window),
        grid=(out_len // chunk, groups),
        in_specs=[
            pl.BlockSpec((group, full), lambda c, g: (g, 0)),
            pl.BlockSpec((window // LANES, group * slots, LANES), lambda c, g: (0, g, 0)),
            pl.BlockSpec((slots, lanes), lambda c, g: (0, 0)),
        ],
        out_specs=pl.BlockSpec((chunk // LANES, slots, LANES), lambda c, g: (c, 0, 0)),
        out_shape=jax.ShapeDtypeStruct((out_len // LANES, slots, LANES), jnp.float32),
        scratch_shapes=[
            pltpu.VMEM((length // LANES, group * ROWS, LANES), jnp.float32),
            pltpu.VMEM((2, LANES, length - LANES), jnp.bfloat16),
            pltpu.VMEM((group, chunk), jnp.float32),
        ],
        name="station_sums",
    )(stream, temps, weights)


def enter(peers):
    barrier = pltpu.get_barrier_semaphore()
    for peer in peers:
        pl.semaphore_signal(barrier, inc=1, device_id=peer, device_id_type=pl.DeviceIdType.MESH)
    pl.semaphore_wait(barrier, len(peers))


def collect_rows(
    count, ids_ref, records_ref, following_ref, library_ref, mask_ref, group_ref,
    stream_ref, temps_ref, weights_ref, held, tail, templates, own_sem, send_sem, recv_sem,
):
    me = lax.axis_index("tm")
    pull = pltpu.make_async_copy(library_ref, templates, own_sem.at[2])
    pull.start()
    rows, block_len = held.shape[1:]
    offset = pl.multiple_of(me * rows, rows)
    own = pltpu.make_async_copy(records_ref.at[pl.ds(offset, rows), :], held.at[me], own_sem.at[0])
    after = pltpu.make_async_copy(following_ref.at[pl.ds(offset, rows), :], tail, own_sem.at[1])
    own.start()
    after.start()
    others = [lax.rem(me + step, count) for step in range(1, count)]
    enter([{"tm": other} for other in others])
    copies = []
    for step, other in enumerate(others):
        copy = pltpu.make_async_remote_copy(
            src_ref=records_ref.at[pl.ds(pl.multiple_of(other * rows, rows), rows), :],
            dst_ref=held.at[me],
            send_sem=send_sem.at[step],
            recv_sem=recv_sem.at[step],
            device_id={"tm": other},
            device_id_type=pl.DeviceIdType.MESH,
        )
        copy.start()
        copies.append(copy)
    after.wait()
    out_len = count * block_len
    stream_ref[:, out_len:] = jnp.zeros((rows, stream_ref.shape[1] - out_len), jnp.float32)
    stream_ref[:, out_len : out_len + tail.shape[1]] = tail[...].astype(jnp.float32)

    stations = mask_ref.shape[1]
    slots, lanes = weights_ref.shape
    window = templates.shape[2]
    first = lax.axis_index("sta") * (rows * count) + offset
    turn = lax.rem(stations - first, stations)
    mask = jnp.concatenate([mask_ref[pl.ds(ids_ref[j], 1), :] for j in range(slots)], axis=0)
    mask = mask.astype(jnp.float32)
    names = group_ref[...]
    onehot = lax.broadcasted_iota(jnp.int32, (G, stations), 0) == jnp.broadcast_to(names, (G, stations))
    counts = lax.dot_general(
        mask.astype(jnp.bfloat16),
        onehot.astype(jnp.float32).astype(jnp.bfloat16),
        (((1,), (1,)), ((), ())),
        preferred_element_type=jnp.float32,
    )
    mine = pltpu.roll(jnp.broadcast_to(names, (8, stations)), turn, 1)[:1, :lanes]
    chosen = lax.broadcasted_iota(jnp.int32, (G, lanes), 0) == jnp.broadcast_to(mine, (G, lanes))
    chosen = chosen.astype(jnp.float32).astype(jnp.bfloat16)
    high = jnp.floor(counts / 128.0) * 128.0
    low = counts - high
    per_station = jnp.dot(high.astype(jnp.bfloat16), chosen, preferred_element_type=jnp.float32) + jnp.dot(
        low.astype(jnp.bfloat16), chosen, preferred_element_type=jnp.float32
    )
    my_mask = pltpu.roll(mask, turn, 1)[:, :lanes]
    weights_ref[...] = my_mask * lax.rsqrt(jnp.float32(window * G) * jnp.maximum(per_station, 1.0))

    pull.wait()
    for j in range(slots):
        template = templates[ids_ref[j]].astype(jnp.float32)
        for block in range(window // LANES):
            temps_ref[block, pl.ds(j, rows, stride=slots), :] = template[:, block * LANES : (block + 1) * LANES]

    own.wait()
    for copy in copies:
        copy.wait()
    for block in range(count):
        stream_ref[:, block * block_len : (block + 1) * block_len] = held[block].astype(jnp.float32)


def collect_stream(flat_ids, records, following, library, channel_mask, station_group, count):
    sta_rows, block_len = records.shape
    rows, window = library.shape[1:]
    slots = flat_ids.shape[0]
    lanes = -(-rows // LANES) * LANES
    return pl.pallas_call(
        functools.partial(collect_rows, count),
        in_specs=[pl.BlockSpec(memory_space=pltpu.SMEM)]
        + [pl.BlockSpec(memory_space=pl.ANY)] * 3
        + [pl.BlockSpec(memory_space=pltpu.VMEM)] * 2,
        out_specs=[pl.BlockSpec(memory_space=pltpu.VMEM)] * 3,
        out_shape=[
            jax.ShapeDtypeStruct((rows, count * block_len + window), jnp.float32),
            jax.ShapeDtypeStruct((window // LANES, rows * slots, LANES), jnp.float32),
            jax.ShapeDtypeStruct((slots, lanes), jnp.float32),
        ],
        scratch_shapes=[
            pltpu.VMEM((count, rows, block_len), records.dtype),
            pltpu.VMEM((rows, following.shape[1]), following.dtype),
            pltpu.VMEM(library.shape, library.dtype),
            pltpu.SemaphoreType.DMA((3,)),
            pltpu.SemaphoreType.DMA((count - 1,)),
            pltpu.SemaphoreType.DMA((count - 1,)),
        ],
        compiler_params=pltpu.CompilerParams(collective_id=0, has_side_effects=True),
        name="collect_stream",
    )(flat_ids, records, following, library, channel_mask, station_group.reshape(1, -1))


def reduce_blocks(parts_ref, out_ref, held, send_sem, recv_sem):
    blocks, halves = parts_ref.shape[0], parts_ref.shape[1]
    count = blocks * halves
    block, half = lax.axis_index("tm"), lax.axis_index("sta")
    me = block * halves + half
    others = []
    for step in range(1, count):
        other = lax.rem(me + step, count)
        others.append((other // halves, lax.rem(other, halves)))
    enter([{"tm": b, "sta": h} for b, h in others])
    copies = []
    for step, (b, h) in enumerate(others):
        copy = pltpu.make_async_remote_copy(
            src_ref=parts_ref.at[b, h],
            dst_ref=held.at[step],
            send_sem=send_sem.at[step],
            recv_sem=recv_sem.at[step],
            device_id={"tm": b, "sta": h},
            device_id_type=pl.DeviceIdType.MESH,
        )
        copy.start()
        copies.append(copy)
    total = parts_ref[block, half]
    for step, copy in enumerate(copies):
        copy.wait_recv()
        total = total + held[step]
    out_ref[...] = total
    for copy in copies:
        copy.wait_send()


def reduce_parts(parts):
    count = parts.shape[0] * parts.shape[1]
    return pl.pallas_call(
        reduce_blocks,
        in_specs=[pl.BlockSpec(memory_space=pltpu.VMEM)],
        out_specs=pl.BlockSpec(memory_space=pltpu.VMEM),
        out_shape=jax.ShapeDtypeStruct(parts.shape[2:], parts.dtype),
        scratch_shapes=[
            pltpu.VMEM((count - 1,) + parts.shape[2:], parts.dtype),
            pltpu.SemaphoreType.DMA((count - 1,)),
            pltpu.SemaphoreType.DMA((count - 1,)),
        ],
        compiler_params=pltpu.CompilerParams(collective_id=1, has_side_effects=True),
        name="reduce_parts",
    )(parts)


def shards(blocks, halves, records, following, library, template_ids, channel_mask, station_group):
    sta_rows, block_len = records.shape
    batches, per_batch = template_ids.shape
    stream, temps, weights = collect_stream(
        template_ids.reshape(-1), records, following, library, channel_mask, station_group, blocks
    )
    sums = station_sums(stream, temps, weights, blocks * block_len)
    tiles = block_len // LANES
    parts = sums.reshape(blocks, tiles, halves, batches // halves * per_batch, LANES)
    parts = jnp.swapaxes(parts, 1, 2).reshape(blocks, halves, -1, LANES)
    mine = reduce_parts(parts).reshape(tiles, batches // halves, per_batch, LANES)
    return jnp.moveaxis(mine, 0, 2).reshape(batches // halves, per_batch, block_len)


def solution(mesh):
    placed = (
        P("sta", ("days", "tm")),
        P("sta", "days"),
        P(None, ("sta", "tm"), None),
        P(),
        P(),
        P(),
    )
    return jax.shard_map(
        functools.partial(shards, mesh.shape["tm"], mesh.shape["sta"]),
        mesh=mesh,
        in_specs=placed,
        out_specs=P("sta", None, ("days", "tm")),
        check_vma=False,
    )
```

```python
import functools

import jax
import jax.numpy as jnp
from jax import lax
from jax.experimental import pallas as pl
from jax.experimental.pallas import tpu as pltpu
from jax.sharding import PartitionSpec as P

G = 128
LANES = 128
ROWS = 16


epsilon = 1e-06


def correlate_group(chunk, window, stream_ref, temps_ref, weights_ref, out_ref, base, hankel, scale):
    length = chunk + window
    group = stream_ref.shape[0]
    start = pl.multiple_of(pl.program_id(0) * chunk, LANES)
    rows = stream_ref[:, pl.ds(start, length)]

    total = rows * rows
    span = 1
    while span < LANES:
        total = total + pltpu.roll(total, length - span, 1)
        span *= 2
    energy = total[:, :chunk]
    for step in range(1, window // LANES):
        energy = energy + total[:, step * LANES : step * LANES + chunk]
    scale[...] = lax.rsqrt(energy / window + epsilon)

    base[...] = pltpu.roll(rows, length - (ROWS - 1), 1)

    wide = length - LANES
    slots, lanes = weights_ref.shape
    turn = lax.rem(lanes - pl.program_id(1) * group, lanes)
    weights = pltpu.roll(weights_ref[...], turn, 1)
    acc = None
    for s in range(group):
        template = [temps_ref[block, s * slots : (s + 1) * slots, :] for block in range(window // LANES)]
        squares = sum(piece * piece for piece in template)
        tmean = jnp.sum(squares, axis=1, keepdims=True) / window
        weight = weights[:, s : s + 1] * lax.rsqrt(tmean + epsilon)
        template = jnp.concatenate(template, axis=1).astype(jnp.bfloat16)
        slot = s % hankel.shape[0]
        shifted = pltpu.roll(
            jnp.broadcast_to(base[s : s + 1, :], (ROWS, length)), 0, 1, stride=1, stride_axis=0
        ).astype(jnp.bfloat16)
        for part in range(LANES // ROWS):
            hankel[slot, part * ROWS : (part + 1) * ROWS, :] = shifted[:, part * ROWS : part * ROWS + wide]
        matrix = jnp.concatenate(
            [hankel[slot, :, step * LANES : step * LANES + chunk] for step in range(window // LANES)], axis=0
        )
        corr = jnp.dot(template, matrix, preferred_element_type=jnp.float32)
        term = corr * scale[s : s + 1, :] * weight
        acc = term if acc is None else acc + term

    parts = [acc[:, block * LANES : (block + 1) * LANES] for block in range(chunk // LANES)]

    @pl.when(pl.program_id(1) == 0)
    def _():
        for block, part in enumerate(parts):
            out_ref[block] = part

    @pl.when(pl.program_id(1) != 0)
    def _():
        for block, part in enumerate(parts):
            out_ref[block] += part


def station_sums(stream, temps, weights, out_len):
    stations = stream.shape[0]
    slots, lanes = weights.shape
    window = temps.shape[0] * LANES
    group = min(16, stations)
    chunk = min(1024, out_len)
    length = chunk + window
    full = stream.shape[1]
    groups = stations // group
    return pl.pallas_call(
        functools.partial(correlate_group, chunk, window),
        grid=(out_len // chunk, groups),
        in_specs=[
            pl.BlockSpec((group, full), lambda c, g: (g, 0)),
            pl.BlockSpec((window // LANES, group * slots, LANES), lambda c, g: (0, g, 0)),
            pl.BlockSpec((slots, lanes), lambda c, g: (0, 0)),
        ],
        out_specs=pl.BlockSpec((chunk // LANES, slots, LANES), lambda c, g: (c, 0, 0)),
        out_shape=jax.ShapeDtypeStruct((out_len // LANES, slots, LANES), jnp.float32),
        scratch_shapes=[
            pltpu.VMEM((group, length), jnp.float32),
            pltpu.VMEM((2, LANES, length - LANES), jnp.bfloat16),
            pltpu.VMEM((group, chunk), jnp.float32),
        ],
        name="station_sums",
    )(stream, temps, weights)


def enter(peers):
    barrier = pltpu.get_barrier_semaphore()
    for peer in peers:
        pl.semaphore_signal(barrier, inc=1, device_id=peer, device_id_type=pl.DeviceIdType.MESH)
    pl.semaphore_wait(barrier, len(peers))


def collect_rows(
    count, ids_ref, records_ref, following_ref, library_ref, mask_ref, group_ref,
    stream_ref, temps_ref, weights_ref, held, tail, templates, own_sem, send_sem, recv_sem,
):
    me = lax.axis_index("tm")
    pull = pltpu.make_async_copy(library_ref, templates, own_sem.at[2])
    pull.start()
    rows, block_len = held.shape[1:]
    offset = pl.multiple_of(me * rows, rows)
    own = pltpu.make_async_copy(records_ref.at[pl.ds(offset, rows), :], held.at[me], own_sem.at[0])
    after = pltpu.make_async_copy(following_ref.at[pl.ds(offset, rows), :], tail, own_sem.at[1])
    own.start()
    after.start()
    others = [lax.rem(me + step, count) for step in range(1, count)]
    enter([{"tm": other} for other in others])
    copies = []
    for step, other in enumerate(others):
        copy = pltpu.make_async_remote_copy(
            src_ref=records_ref.at[pl.ds(pl.multiple_of(other * rows, rows), rows), :],
            dst_ref=held.at[me],
            send_sem=send_sem.at[step],
            recv_sem=recv_sem.at[step],
            device_id={"tm": other},
            device_id_type=pl.DeviceIdType.MESH,
        )
        copy.start()
        copies.append(copy)
    after.wait()
    out_len = count * block_len
    stream_ref[:, out_len:] = jnp.zeros((rows, stream_ref.shape[1] - out_len), jnp.float32)
    stream_ref[:, out_len : out_len + tail.shape[1]] = tail[...].astype(jnp.float32)

    stations = mask_ref.shape[1]
    slots, lanes = weights_ref.shape
    window = templates.shape[2]
    first = lax.axis_index("sta") * (rows * count) + offset
    turn = lax.rem(stations - first, stations)
    ids = [ids_ref[j // ids_ref.shape[1], j % ids_ref.shape[1]] for j in range(slots)]
    mask = jnp.concatenate([mask_ref[pl.ds(ids[j], 1), :] for j in range(slots)], axis=0)
    mask = mask.astype(jnp.float32)
    names = group_ref[...]
    onehot = lax.broadcasted_iota(jnp.int32, (G, stations), 0) == jnp.broadcast_to(names, (G, stations))
    counts = lax.dot_general(
        mask.astype(jnp.bfloat16),
        onehot.astype(jnp.float32).astype(jnp.bfloat16),
        (((1,), (1,)), ((), ())),
        preferred_element_type=jnp.float32,
    )
    mine = pltpu.roll(jnp.broadcast_to(names, (8, stations)), turn, 1)[:1, :lanes]
    chosen = lax.broadcasted_iota(jnp.int32, (G, lanes), 0) == jnp.broadcast_to(mine, (G, lanes))
    chosen = chosen.astype(jnp.float32).astype(jnp.bfloat16)
    high = jnp.floor(counts / 128.0) * 128.0
    low = counts - high
    per_station = jnp.dot(high.astype(jnp.bfloat16), chosen, preferred_element_type=jnp.float32) + jnp.dot(
        low.astype(jnp.bfloat16), chosen, preferred_element_type=jnp.float32
    )
    my_mask = pltpu.roll(mask, turn, 1)[:, :lanes]
    weights_ref[...] = my_mask * lax.rsqrt(jnp.float32(window * G) * jnp.maximum(per_station, 1.0))

    order = lax.broadcasted_iota(jnp.int32, (window, window), 1) ^ (ROWS - 1)
    turned = (lax.broadcasted_iota(jnp.int32, (window, window), 0) == order)
    turned = turned.astype(jnp.float32).astype(jnp.bfloat16)
    pull.wait()
    for j in range(slots):
        template = jnp.dot(templates[ids[j]], turned, preferred_element_type=jnp.float32)
        for block in range(window // LANES):
            temps_ref[block, pl.ds(j, rows, stride=slots), :] = template[:, block * LANES : (block + 1) * LANES]

    own.wait()
    for copy in copies:
        copy.wait()
    for block in range(count):
        stream_ref[:, block * block_len : (block + 1) * block_len] = held[block].astype(jnp.float32)


def collect_stream(template_ids, records, following, library, channel_mask, station_group, count):
    sta_rows, block_len = records.shape
    rows, window = library.shape[1:]
    slots = template_ids.size
    lanes = -(-rows // LANES) * LANES
    return pl.pallas_call(
        functools.partial(collect_rows, count),
        in_specs=[pl.BlockSpec(memory_space=pltpu.SMEM)]
        + [pl.BlockSpec(memory_space=pl.ANY)] * 3
        + [pl.BlockSpec(memory_space=pltpu.VMEM)] * 2,
        out_specs=[pl.BlockSpec(memory_space=pltpu.VMEM)] * 3,
        out_shape=[
            jax.ShapeDtypeStruct((rows, count * block_len + window), jnp.float32),
            jax.ShapeDtypeStruct((window // LANES, rows * slots, LANES), jnp.float32),
            jax.ShapeDtypeStruct((slots, lanes), jnp.float32),
        ],
        scratch_shapes=[
            pltpu.VMEM((count, rows, block_len), records.dtype),
            pltpu.VMEM((rows, following.shape[1]), following.dtype),
            pltpu.VMEM(library.shape, library.dtype),
            pltpu.SemaphoreType.DMA((3,)),
            pltpu.SemaphoreType.DMA((count - 1,)),
            pltpu.SemaphoreType.DMA((count - 1,)),
        ],
        compiler_params=pltpu.CompilerParams(collective_id=0, has_side_effects=True),
        name="collect_stream",
    )(template_ids, records, following, library, channel_mask, station_group.reshape(1, -1))


def reduce_blocks(parts_ref, out_ref, held, send_sem, recv_sem):
    blocks, halves = parts_ref.shape[0], parts_ref.shape[1]
    count = blocks * halves
    block, half = lax.axis_index("tm"), lax.axis_index("sta")
    me = block * halves + half
    others = []
    for step in range(1, count):
        other = lax.rem(me + step, count)
        others.append((other // halves, lax.rem(other, halves)))
    enter([{"tm": b, "sta": h} for b, h in others])
    copies = []
    for step, (b, h) in enumerate(others):
        copy = pltpu.make_async_remote_copy(
            src_ref=parts_ref.at[b, h],
            dst_ref=held.at[step],
            send_sem=send_sem.at[step],
            recv_sem=recv_sem.at[step],
            device_id={"tm": b, "sta": h},
            device_id_type=pl.DeviceIdType.MESH,
        )
        copy.start()
        copies.append(copy)
    total = parts_ref[block, half]
    for step, copy in enumerate(copies):
        copy.wait_recv()
        total = total + held[step]
    out_ref[...] = total
    for copy in copies:
        copy.wait_send()


def reduce_parts(parts):
    count = parts.shape[0] * parts.shape[1]
    return pl.pallas_call(
        reduce_blocks,
        in_specs=[pl.BlockSpec(memory_space=pltpu.VMEM)],
        out_specs=pl.BlockSpec(memory_space=pltpu.VMEM),
        out_shape=jax.ShapeDtypeStruct(parts.shape[2:], parts.dtype),
        scratch_shapes=[
            pltpu.VMEM((count - 1,) + parts.shape[2:], parts.dtype),
            pltpu.SemaphoreType.DMA((count - 1,)),
            pltpu.SemaphoreType.DMA((count - 1,)),
        ],
        compiler_params=pltpu.CompilerParams(collective_id=1, has_side_effects=True),
        name="reduce_parts",
    )(parts)


def shards(blocks, halves, records, following, library, template_ids, channel_mask, station_group):
    sta_rows, block_len = records.shape
    batches, per_batch = template_ids.shape
    stream, temps, weights = collect_stream(
        template_ids, records, following, library, channel_mask, station_group, blocks
    )
    sums = station_sums(stream, temps, weights, blocks * block_len)
    tiles = block_len // LANES
    parts = sums.reshape(blocks, tiles, halves, batches // halves * per_batch, LANES)
    parts = jnp.swapaxes(parts, 1, 2).reshape(blocks, halves, -1, LANES)
    mine = reduce_parts(parts).reshape(tiles, batches // halves, per_batch, LANES)
    return jnp.moveaxis(mine, 0, 2).reshape(batches // halves, per_batch, block_len)


def solution(mesh):
    placed = (
        P("sta", ("days", "tm")),
        P("sta", "days"),
        P(None, ("sta", "tm"), None),
        P(),
        P(),
        P(),
    )
    return jax.shard_map(
        functools.partial(shards, mesh.shape["tm"], mesh.shape["sta"]),
        mesh=mesh,
        in_specs=placed,
        out_specs=P("sta", None, ("days", "tm")),
        check_vma=False,
    )
```

```python
import functools

import jax
import jax.numpy as jnp
from jax import lax
from jax.experimental import pallas as pl
from jax.experimental.pallas import tpu as pltpu
from jax.sharding import PartitionSpec as P

G = 128
LANES = 128
ROWS = 16


epsilon = 1e-06


def correlate_group(chunk, window, stream_ref, temps_ref, weights_ref, out_ref, ahead, base, hankel, scale):
    length = chunk + window
    group = stream_ref.shape[0]
    start = pl.multiple_of(pl.program_id(0) * chunk, LANES)
    rows = stream_ref[:, pl.ds(start, length)]

    total = rows * rows
    span = 1
    while span < LANES:
        total = total + pltpu.roll(total, length - span, 1)
        span *= 2
    energy = total[:, :chunk]
    for step in range(1, window // LANES):
        energy = energy + total[:, step * LANES : step * LANES + chunk]
    scale[...] = lax.rsqrt(energy / window + epsilon)

    ahead[...] = pltpu.roll(rows, length - (ROWS - 1), 1)
    batch = min(8, group)

    def turn_rows(step, carry):
        for k in range(batch):
            s = step * batch + k
            row = jnp.broadcast_to(ahead[pl.ds(s, 1), :], (ROWS, length))
            base[s] = pltpu.roll(row, 0, 1, stride=1, stride_axis=0).astype(base.dtype)
        return carry

    lax.fori_loop(0, group // batch, turn_rows, 0)

    wide = length - LANES
    slots, lanes = weights_ref.shape
    turn = lax.rem(lanes - pl.program_id(1) * group, lanes)
    weights = pltpu.roll(weights_ref[...], turn, 1)
    acc = None
    for s in range(group):
        template = [temps_ref[block, s * slots : (s + 1) * slots, :] for block in range(window // LANES)]
        squares = sum(piece * piece for piece in template)
        tmean = jnp.sum(squares, axis=1, keepdims=True) / window
        weight = weights[:, s : s + 1] * lax.rsqrt(tmean + epsilon)
        template = jnp.concatenate(template, axis=1).astype(jnp.bfloat16)
        slot = s % hankel.shape[0]
        shifted = base[s].astype(jnp.bfloat16)
        for part in range(LANES // ROWS):
            hankel[slot, part * ROWS : (part + 1) * ROWS, :] = shifted[:, part * ROWS : part * ROWS + wide]
        matrix = jnp.concatenate(
            [hankel[slot, :, step * LANES : step * LANES + chunk] for step in range(window // LANES)], axis=0
        )
        corr = jnp.dot(template, matrix, preferred_element_type=jnp.float32)
        term = corr * scale[s : s + 1, :] * weight
        acc = term if acc is None else acc + term

    parts = [acc[:, block * LANES : (block + 1) * LANES] for block in range(chunk // LANES)]

    @pl.when(pl.program_id(1) == 0)
    def _():
        for block, part in enumerate(parts):
            out_ref[block] = part

    @pl.when(pl.program_id(1) != 0)
    def _():
        for block, part in enumerate(parts):
            out_ref[block] += part


def station_sums(stream, temps, weights, out_len):
    stations = stream.shape[0]
    slots, lanes = weights.shape
    window = temps.shape[0] * LANES
    group = min(16, stations)
    chunk = min(1024, out_len)
    length = chunk + window
    full = stream.shape[1]
    groups = stations // group
    return pl.pallas_call(
        functools.partial(correlate_group, chunk, window),
        grid=(out_len // chunk, groups),
        in_specs=[
            pl.BlockSpec((group, full), lambda c, g: (g, 0)),
            pl.BlockSpec((window // LANES, group * slots, LANES), lambda c, g: (0, g, 0)),
            pl.BlockSpec((slots, lanes), lambda c, g: (0, 0)),
        ],
        out_specs=pl.BlockSpec((chunk // LANES, slots, LANES), lambda c, g: (c, 0, 0)),
        out_shape=jax.ShapeDtypeStruct((out_len // LANES, slots, LANES), jnp.float32),
        scratch_shapes=[
            pltpu.VMEM((group, length), jnp.float32),
            pltpu.VMEM((group, ROWS, length), jnp.bfloat16),
            pltpu.VMEM((2, LANES, length - LANES), jnp.bfloat16),
            pltpu.VMEM((group, chunk), jnp.float32),
        ],
        name="station_sums",
    )(stream, temps, weights)


def enter(peers):
    barrier = pltpu.get_barrier_semaphore()
    for peer in peers:
        pl.semaphore_signal(barrier, inc=1, device_id=peer, device_id_type=pl.DeviceIdType.MESH)
    pl.semaphore_wait(barrier, len(peers))


def collect_rows(
    count, ids_ref, records_ref, following_ref, library_ref, mask_ref, group_ref,
    stream_ref, temps_ref, weights_ref, held, tail, templates, own_sem, send_sem, recv_sem,
):
    me = lax.axis_index("tm")
    pull = pltpu.make_async_copy(library_ref, templates, own_sem.at[2])
    pull.start()
    rows, block_len = held.shape[1:]
    offset = pl.multiple_of(me * rows, rows)
    own = pltpu.make_async_copy(records_ref.at[pl.ds(offset, rows), :], held.at[me], own_sem.at[0])
    after = pltpu.make_async_copy(following_ref.at[pl.ds(offset, rows), :], tail, own_sem.at[1])
    own.start()
    after.start()
    others = [lax.rem(me + step, count) for step in range(1, count)]
    enter([{"tm": other} for other in others])
    copies = []
    for step, other in enumerate(others):
        copy = pltpu.make_async_remote_copy(
            src_ref=records_ref.at[pl.ds(pl.multiple_of(other * rows, rows), rows), :],
            dst_ref=held.at[me],
            send_sem=send_sem.at[step],
            recv_sem=recv_sem.at[step],
            device_id={"tm": other},
            device_id_type=pl.DeviceIdType.MESH,
        )
        copy.start()
        copies.append(copy)
    after.wait()
    out_len = count * block_len
    stream_ref[:, out_len:] = jnp.zeros((rows, stream_ref.shape[1] - out_len), jnp.float32)
    stream_ref[:, out_len : out_len + tail.shape[1]] = tail[...].astype(jnp.float32)

    stations = mask_ref.shape[1]
    slots, lanes = weights_ref.shape
    window = templates.shape[2]
    first = lax.axis_index("sta") * (rows * count) + offset
    turn = lax.rem(stations - first, stations)
    ids = [ids_ref[j // ids_ref.shape[1], j % ids_ref.shape[1]] for j in range(slots)]
    mask = jnp.concatenate([mask_ref[pl.ds(ids[j], 1), :] for j in range(slots)], axis=0)
    mask = mask.astype(jnp.float32)
    names = group_ref[...]
    onehot = lax.broadcasted_iota(jnp.int32, (G, stations), 0) == jnp.broadcast_to(names, (G, stations))
    counts = lax.dot_general(
        mask.astype(jnp.bfloat16),
        onehot.astype(jnp.float32).astype(jnp.bfloat16),
        (((1,), (1,)), ((), ())),
        preferred_element_type=jnp.float32,
    )
    mine = pltpu.roll(jnp.broadcast_to(names, (8, stations)), turn, 1)[:1, :lanes]
    chosen = lax.broadcasted_iota(jnp.int32, (G, lanes), 0) == jnp.broadcast_to(mine, (G, lanes))
    chosen = chosen.astype(jnp.float32).astype(jnp.bfloat16)
    high = jnp.floor(counts / 128.0) * 128.0
    low = counts - high
    per_station = jnp.dot(high.astype(jnp.bfloat16), chosen, preferred_element_type=jnp.float32) + jnp.dot(
        low.astype(jnp.bfloat16), chosen, preferred_element_type=jnp.float32
    )
    my_mask = pltpu.roll(mask, turn, 1)[:, :lanes]
    weights_ref[...] = my_mask * lax.rsqrt(jnp.float32(window * G) * jnp.maximum(per_station, 1.0))

    order = lax.broadcasted_iota(jnp.int32, (window, window), 1) ^ (ROWS - 1)
    turned = (lax.broadcasted_iota(jnp.int32, (window, window), 0) == order)
    turned = turned.astype(jnp.float32).astype(jnp.bfloat16)
    pull.wait()
    for j in range(slots):
        template = jnp.dot(templates[ids[j]], turned, preferred_element_type=jnp.float32)
        for block in range(window // LANES):
            temps_ref[block, pl.ds(j, rows, stride=slots), :] = template[:, block * LANES : (block + 1) * LANES]

    own.wait()
    for copy in copies:
        copy.wait()
    for block in range(count):
        stream_ref[:, block * block_len : (block + 1) * block_len] = held[block].astype(jnp.float32)


def collect_stream(template_ids, records, following, library, channel_mask, station_group, count):
    sta_rows, block_len = records.shape
    rows, window = library.shape[1:]
    slots = template_ids.size
    lanes = -(-rows // LANES) * LANES
    return pl.pallas_call(
        functools.partial(collect_rows, count),
        in_specs=[pl.BlockSpec(memory_space=pltpu.SMEM)]
        + [pl.BlockSpec(memory_space=pl.ANY)] * 3
        + [pl.BlockSpec(memory_space=pltpu.VMEM)] * 2,
        out_specs=[pl.BlockSpec(memory_space=pltpu.VMEM)] * 3,
        out_shape=[
            jax.ShapeDtypeStruct((rows, count * block_len + window), jnp.float32),
            jax.ShapeDtypeStruct((window // LANES, rows * slots, LANES), jnp.float32),
            jax.ShapeDtypeStruct((slots, lanes), jnp.float32),
        ],
        scratch_shapes=[
            pltpu.VMEM((count, rows, block_len), records.dtype),
            pltpu.VMEM((rows, following.shape[1]), following.dtype),
            pltpu.VMEM(library.shape, library.dtype),
            pltpu.SemaphoreType.DMA((3,)),
            pltpu.SemaphoreType.DMA((count - 1,)),
            pltpu.SemaphoreType.DMA((count - 1,)),
        ],
        compiler_params=pltpu.CompilerParams(collective_id=0, has_side_effects=True),
        name="collect_stream",
    )(template_ids, records, following, library, channel_mask, station_group.reshape(1, -1))


def reduce_blocks(parts_ref, out_ref, held, send_sem, recv_sem):
    blocks, halves = parts_ref.shape[0], parts_ref.shape[1]
    count = blocks * halves
    block, half = lax.axis_index("tm"), lax.axis_index("sta")
    me = block * halves + half
    others = []
    for step in range(1, count):
        other = lax.rem(me + step, count)
        others.append((other // halves, lax.rem(other, halves)))
    enter([{"tm": b, "sta": h} for b, h in others])
    copies = []
    for step, (b, h) in enumerate(others):
        copy = pltpu.make_async_remote_copy(
            src_ref=parts_ref.at[b, h],
            dst_ref=held.at[step],
            send_sem=send_sem.at[step],
            recv_sem=recv_sem.at[step],
            device_id={"tm": b, "sta": h},
            device_id_type=pl.DeviceIdType.MESH,
        )
        copy.start()
        copies.append(copy)
    total = parts_ref[block, half]
    for step, copy in enumerate(copies):
        copy.wait_recv()
        total = total + held[step]
    out_ref[...] = total
    for copy in copies:
        copy.wait_send()


def reduce_parts(parts):
    count = parts.shape[0] * parts.shape[1]
    return pl.pallas_call(
        reduce_blocks,
        in_specs=[pl.BlockSpec(memory_space=pltpu.VMEM)],
        out_specs=pl.BlockSpec(memory_space=pltpu.VMEM),
        out_shape=jax.ShapeDtypeStruct(parts.shape[2:], parts.dtype),
        scratch_shapes=[
            pltpu.VMEM((count - 1,) + parts.shape[2:], parts.dtype),
            pltpu.SemaphoreType.DMA((count - 1,)),
            pltpu.SemaphoreType.DMA((count - 1,)),
        ],
        compiler_params=pltpu.CompilerParams(collective_id=1, has_side_effects=True),
        name="reduce_parts",
    )(parts)


def shards(blocks, halves, records, following, library, template_ids, channel_mask, station_group):
    sta_rows, block_len = records.shape
    batches, per_batch = template_ids.shape
    stream, temps, weights = collect_stream(
        template_ids, records, following, library, channel_mask, station_group, blocks
    )
    sums = station_sums(stream, temps, weights, blocks * block_len)
    tiles = block_len // LANES
    parts = sums.reshape(blocks, tiles, halves, batches // halves * per_batch, LANES)
    parts = jnp.swapaxes(parts, 1, 2).reshape(blocks, halves, -1, LANES)
    mine = reduce_parts(parts).reshape(tiles, batches // halves, per_batch, LANES)
    return jnp.moveaxis(mine, 0, 2).reshape(batches // halves, per_batch, block_len)


def solution(mesh):
    placed = (
        P("sta", ("days", "tm")),
        P("sta", "days"),
        P(None, ("sta", "tm"), None),
        P(),
        P(),
        P(),
    )
    return jax.shard_map(
        functools.partial(shards, mesh.shape["tm"], mesh.shape["sta"]),
        mesh=mesh,
        in_specs=placed,
        out_specs=P("sta", None, ("days", "tm")),
        check_vma=False,
    )
```

```python
import functools

import jax
import jax.numpy as jnp
from jax import lax
from jax.experimental import pallas as pl
from jax.experimental.pallas import tpu as pltpu
from jax.sharding import PartitionSpec as P

G = 128
LANES = 128
ROWS = 16


epsilon = 1e-06


def correlate_group(chunk, window, stream_ref, temps_ref, weights_ref, out_ref, ahead, base, hankel, scale):
    length = chunk + window
    group = stream_ref.shape[0]
    start = pl.multiple_of(pl.program_id(0) * chunk, LANES)
    rows = stream_ref[:, pl.ds(start, length)]

    ahead[...] = pltpu.roll(rows, length - (ROWS - 1), 1)
    batch = min(8, group)

    def turn_rows(step, carry):
        for k in range(batch):
            s = step * batch + k
            row = jnp.broadcast_to(ahead[pl.ds(s, 1), :], (ROWS, length))
            base[s] = pltpu.roll(row, 0, 1, stride=1, stride_axis=0).astype(base.dtype)
        return carry

    lax.fori_loop(0, group // batch, turn_rows, 0)

    square = rows * rows
    high = square.astype(jnp.bfloat16)
    low = (square - high.astype(jnp.float32)).astype(jnp.bfloat16)
    depth = window + LANES
    late = lax.broadcasted_iota(jnp.int32, (depth, LANES), 0) - lax.broadcasted_iota(jnp.int32, (depth, LANES), 1)
    band = jnp.logical_and(late >= 0, late < window).astype(jnp.float32).astype(jnp.bfloat16)
    frames = [
        half[:, block * LANES : block * LANES + depth] for half in (high, low) for block in range(chunk // LANES)
    ]
    sums = jnp.dot(jnp.concatenate(frames, axis=0), band, preferred_element_type=jnp.float32)
    sums = sums[: sums.shape[0] // 2] + sums[sums.shape[0] // 2 :]
    for block in range(chunk // LANES):
        energy = sums[block * group : (block + 1) * group] / window
        scale[:, block * LANES : (block + 1) * LANES] = lax.rsqrt(energy + epsilon)

    wide = length - LANES
    slots, lanes = weights_ref.shape
    turn = lax.rem(lanes - pl.program_id(1) * group, lanes)
    weights = pltpu.roll(weights_ref[...], turn, 1)
    acc = None
    for s in range(group):
        template = [temps_ref[block, s * slots : (s + 1) * slots, :] for block in range(window // LANES)]
        squares = sum(piece * piece for piece in template)
        tmean = jnp.sum(squares, axis=1, keepdims=True) / window
        weight = weights[:, s : s + 1] * lax.rsqrt(tmean + epsilon)
        template = jnp.concatenate(template, axis=1).astype(jnp.bfloat16)
        slot = s % hankel.shape[0]
        shifted = base[s].astype(jnp.bfloat16)
        for part in range(LANES // ROWS):
            hankel[slot, part * ROWS : (part + 1) * ROWS, :] = shifted[:, part * ROWS : part * ROWS + wide]
        matrix = jnp.concatenate(
            [hankel[slot, :, step * LANES : step * LANES + chunk] for step in range(window // LANES)], axis=0
        )
        corr = jnp.dot(template, matrix, preferred_element_type=jnp.float32)
        term = corr * scale[s : s + 1, :] * weight
        acc = term if acc is None else acc + term

    parts = [acc[:, block * LANES : (block + 1) * LANES] for block in range(chunk // LANES)]

    @pl.when(pl.program_id(1) == 0)
    def _():
        for block, part in enumerate(parts):
            out_ref[block] = part

    @pl.when(pl.program_id(1) != 0)
    def _():
        for block, part in enumerate(parts):
            out_ref[block] += part


def station_sums(stream, temps, weights, out_len):
    stations = stream.shape[0]
    slots, lanes = weights.shape
    window = temps.shape[0] * LANES
    group = min(16, stations)
    chunk = min(1024, out_len)
    length = chunk + window
    full = stream.shape[1]
    groups = stations // group
    return pl.pallas_call(
        functools.partial(correlate_group, chunk, window),
        grid=(out_len // chunk, groups),
        in_specs=[
            pl.BlockSpec((group, full), lambda c, g: (g, 0)),
            pl.BlockSpec((window // LANES, group * slots, LANES), lambda c, g: (0, g, 0)),
            pl.BlockSpec((slots, lanes), lambda c, g: (0, 0)),
        ],
        out_specs=pl.BlockSpec((chunk // LANES, slots, LANES), lambda c, g: (c, 0, 0)),
        out_shape=jax.ShapeDtypeStruct((out_len // LANES, slots, LANES), jnp.float32),
        scratch_shapes=[
            pltpu.VMEM((group, length), jnp.float32),
            pltpu.VMEM((group, ROWS, length), jnp.bfloat16),
            pltpu.VMEM((2, LANES, length - LANES), jnp.bfloat16),
            pltpu.VMEM((group, chunk), jnp.float32),
        ],
        name="station_sums",
    )(stream, temps, weights)


def enter(peers):
    barrier = pltpu.get_barrier_semaphore()
    for peer in peers:
        pl.semaphore_signal(barrier, inc=1, device_id=peer, device_id_type=pl.DeviceIdType.MESH)
    pl.semaphore_wait(barrier, len(peers))


def collect_rows(
    count, ids_ref, records_ref, following_ref, library_ref, mask_ref, group_ref,
    stream_ref, temps_ref, weights_ref, held, tail, templates, own_sem, send_sem, recv_sem,
):
    me = lax.axis_index("tm")
    pull = pltpu.make_async_copy(library_ref, templates, own_sem.at[2])
    pull.start()
    rows, block_len = held.shape[1:]
    offset = pl.multiple_of(me * rows, rows)
    own = pltpu.make_async_copy(records_ref.at[pl.ds(offset, rows), :], held.at[me], own_sem.at[0])
    after = pltpu.make_async_copy(following_ref.at[pl.ds(offset, rows), :], tail, own_sem.at[1])
    own.start()
    after.start()
    others = [lax.rem(me + step, count) for step in range(1, count)]
    enter([{"tm": other} for other in others])
    copies = []
    for step, other in enumerate(others):
        copy = pltpu.make_async_remote_copy(
            src_ref=records_ref.at[pl.ds(pl.multiple_of(other * rows, rows), rows), :],
            dst_ref=held.at[me],
            send_sem=send_sem.at[step],
            recv_sem=recv_sem.at[step],
            device_id={"tm": other},
            device_id_type=pl.DeviceIdType.MESH,
        )
        copy.start()
        copies.append(copy)
    after.wait()
    out_len = count * block_len
    stream_ref[:, out_len:] = jnp.zeros((rows, stream_ref.shape[1] - out_len), jnp.float32)
    stream_ref[:, out_len : out_len + tail.shape[1]] = tail[...].astype(jnp.float32)

    stations = mask_ref.shape[1]
    slots, lanes = weights_ref.shape
    window = templates.shape[2]
    first = lax.axis_index("sta") * (rows * count) + offset
    turn = lax.rem(stations - first, stations)
    ids = [ids_ref[j // ids_ref.shape[1], j % ids_ref.shape[1]] for j in range(slots)]
    mask = jnp.concatenate([mask_ref[pl.ds(ids[j], 1), :] for j in range(slots)], axis=0)
    mask = mask.astype(jnp.float32)
    names = group_ref[...]
    onehot = lax.broadcasted_iota(jnp.int32, (G, stations), 0) == jnp.broadcast_to(names, (G, stations))
    counts = lax.dot_general(
        mask.astype(jnp.bfloat16),
        onehot.astype(jnp.float32).astype(jnp.bfloat16),
        (((1,), (1,)), ((), ())),
        preferred_element_type=jnp.float32,
    )
    mine = pltpu.roll(jnp.broadcast_to(names, (8, stations)), turn, 1)[:1, :lanes]
    chosen = lax.broadcasted_iota(jnp.int32, (G, lanes), 0) == jnp.broadcast_to(mine, (G, lanes))
    chosen = chosen.astype(jnp.float32).astype(jnp.bfloat16)
    high = jnp.floor(counts / 128.0) * 128.0
    low = counts - high
    per_station = jnp.dot(high.astype(jnp.bfloat16), chosen, preferred_element_type=jnp.float32) + jnp.dot(
        low.astype(jnp.bfloat16), chosen, preferred_element_type=jnp.float32
    )
    my_mask = pltpu.roll(mask, turn, 1)[:, :lanes]
    weights_ref[...] = my_mask * lax.rsqrt(jnp.float32(window * G) * jnp.maximum(per_station, 1.0))

    order = lax.broadcasted_iota(jnp.int32, (window, window), 1) ^ (ROWS - 1)
    turned = (lax.broadcasted_iota(jnp.int32, (window, window), 0) == order)
    turned = turned.astype(jnp.float32).astype(jnp.bfloat16)
    pull.wait()
    for j in range(slots):
        template = jnp.dot(templates[ids[j]], turned, preferred_element_type=jnp.float32)
        for block in range(window // LANES):
            temps_ref[block, pl.ds(j, rows, stride=slots), :] = template[:, block * LANES : (block + 1) * LANES]

    own.wait()
    for copy in copies:
        copy.wait()
    for block in range(count):
        stream_ref[:, block * block_len : (block + 1) * block_len] = held[block].astype(jnp.float32)


def collect_stream(template_ids, records, following, library, channel_mask, station_group, count):
    sta_rows, block_len = records.shape
    rows, window = library.shape[1:]
    slots = template_ids.size
    lanes = -(-rows // LANES) * LANES
    return pl.pallas_call(
        functools.partial(collect_rows, count),
        in_specs=[pl.BlockSpec(memory_space=pltpu.SMEM)]
        + [pl.BlockSpec(memory_space=pl.ANY)] * 3
        + [pl.BlockSpec(memory_space=pltpu.VMEM)] * 2,
        out_specs=[pl.BlockSpec(memory_space=pltpu.VMEM)] * 3,
        out_shape=[
            jax.ShapeDtypeStruct((rows, count * block_len + window), jnp.float32),
            jax.ShapeDtypeStruct((window // LANES, rows * slots, LANES), jnp.float32),
            jax.ShapeDtypeStruct((slots, lanes), jnp.float32),
        ],
        scratch_shapes=[
            pltpu.VMEM((count, rows, block_len), records.dtype),
            pltpu.VMEM((rows, following.shape[1]), following.dtype),
            pltpu.VMEM(library.shape, library.dtype),
            pltpu.SemaphoreType.DMA((3,)),
            pltpu.SemaphoreType.DMA((count - 1,)),
            pltpu.SemaphoreType.DMA((count - 1,)),
        ],
        compiler_params=pltpu.CompilerParams(collective_id=0, has_side_effects=True),
        name="collect_stream",
    )(template_ids, records, following, library, channel_mask, station_group.reshape(1, -1))


def reduce_blocks(parts_ref, out_ref, held, send_sem, recv_sem):
    blocks, halves = parts_ref.shape[0], parts_ref.shape[1]
    count = blocks * halves
    block, half = lax.axis_index("tm"), lax.axis_index("sta")
    me = block * halves + half
    others = []
    for step in range(1, count):
        other = lax.rem(me + step, count)
        others.append((other // halves, lax.rem(other, halves)))
    enter([{"tm": b, "sta": h} for b, h in others])
    copies = []
    for step, (b, h) in enumerate(others):
        copy = pltpu.make_async_remote_copy(
            src_ref=parts_ref.at[b, h],
            dst_ref=held.at[step],
            send_sem=send_sem.at[step],
            recv_sem=recv_sem.at[step],
            device_id={"tm": b, "sta": h},
            device_id_type=pl.DeviceIdType.MESH,
        )
        copy.start()
        copies.append(copy)
    total = parts_ref[block, half]
    for step, copy in enumerate(copies):
        copy.wait_recv()
        total = total + held[step]
    out_ref[...] = total
    for copy in copies:
        copy.wait_send()


def reduce_parts(parts):
    count = parts.shape[0] * parts.shape[1]
    return pl.pallas_call(
        reduce_blocks,
        in_specs=[pl.BlockSpec(memory_space=pltpu.VMEM)],
        out_specs=pl.BlockSpec(memory_space=pltpu.VMEM),
        out_shape=jax.ShapeDtypeStruct(parts.shape[2:], parts.dtype),
        scratch_shapes=[
            pltpu.VMEM((count - 1,) + parts.shape[2:], parts.dtype),
            pltpu.SemaphoreType.DMA((count - 1,)),
            pltpu.SemaphoreType.DMA((count - 1,)),
        ],
        compiler_params=pltpu.CompilerParams(collective_id=1, has_side_effects=True),
        name="reduce_parts",
    )(parts)


def shards(blocks, halves, records, following, library, template_ids, channel_mask, station_group):
    sta_rows, block_len = records.shape
    batches, per_batch = template_ids.shape
    stream, temps, weights = collect_stream(
        template_ids, records, following, library, channel_mask, station_group, blocks
    )
    sums = station_sums(stream, temps, weights, blocks * block_len)
    tiles = block_len // LANES
    parts = sums.reshape(blocks, tiles, halves, batches // halves * per_batch, LANES)
    parts = jnp.swapaxes(parts, 1, 2).reshape(blocks, halves, -1, LANES)
    mine = reduce_parts(parts).reshape(tiles, batches // halves, per_batch, LANES)
    return jnp.moveaxis(mine, 0, 2).reshape(batches // halves, per_batch, block_len)


def solution(mesh):
    placed = (
        P("sta", ("days", "tm")),
        P("sta", "days"),
        P(None, ("sta", "tm"), None),
        P(),
        P(),
        P(),
    )
    return jax.shard_map(
        functools.partial(shards, mesh.shape["tm"], mesh.shape["sta"]),
        mesh=mesh,
        in_specs=placed,
        out_specs=P("sta", None, ("days", "tm")),
        check_vma=False,
    )
```

```python
import functools

import jax
import jax.numpy as jnp
from jax import lax
from jax.experimental import pallas as pl
from jax.experimental.pallas import tpu as pltpu
from jax.sharding import PartitionSpec as P

G = 128
LANES = 128
ROWS = 16


epsilon = 1e-06


def correlate_group(chunk, window, stream_ref, temps_ref, weights_ref, out_ref, ahead, base, hankel, scale):
    length = chunk + window
    group = stream_ref.shape[0]
    start = pl.multiple_of(pl.program_id(0) * chunk, LANES)
    rows = stream_ref[:, pl.ds(start, length)]

    ahead[...] = pltpu.roll(rows, length - (ROWS - 1), 1)
    batch = min(8, group)

    def turn_rows(step, carry):
        for k in range(batch):
            s = step * batch + k
            row = jnp.broadcast_to(ahead[pl.ds(s, 1), :], (ROWS, length))
            base[s] = pltpu.roll(row, 0, 1, stride=1, stride_axis=0).astype(base.dtype)
        return carry

    lax.fori_loop(0, group // batch, turn_rows, 0)

    square = rows * rows
    high = square.astype(jnp.bfloat16)
    low = (square - high.astype(jnp.float32)).astype(jnp.bfloat16)
    depth = window + LANES
    late = lax.broadcasted_iota(jnp.int32, (depth, LANES), 0) - lax.broadcasted_iota(jnp.int32, (depth, LANES), 1)
    band = jnp.logical_and(late >= 0, late < window).astype(jnp.float32).astype(jnp.bfloat16)
    frames = [
        half[:, block * LANES : block * LANES + depth] for half in (high, low) for block in range(chunk // LANES)
    ]
    sums = jnp.dot(jnp.concatenate(frames, axis=0), band, preferred_element_type=jnp.float32)
    sums = sums[: sums.shape[0] // 2] + sums[sums.shape[0] // 2 :]
    for block in range(chunk // LANES):
        energy = sums[block * group : (block + 1) * group] / window
        scale[:, block * LANES : (block + 1) * LANES] = lax.rsqrt(energy + epsilon)

    wide = length - LANES
    slots, lanes = weights_ref.shape
    turn = lax.rem(lanes - pl.program_id(1) * group, lanes)
    weights = pltpu.roll(weights_ref[...], turn, 1)
    acc = None
    for s in range(group):
        template = [temps_ref[block, s * slots : (s + 1) * slots, :] for block in range(window // LANES)]
        squares = sum(piece * piece for piece in template)
        tmean = jnp.sum(squares, axis=1, keepdims=True) / window
        weight = weights[:, s : s + 1] * lax.rsqrt(tmean + epsilon)
        template = jnp.concatenate(template, axis=1).astype(jnp.bfloat16)
        slot = s % hankel.shape[0]
        shifted = base[s].astype(jnp.bfloat16)
        for part in range(LANES // ROWS):
            hankel[slot, part * ROWS : (part + 1) * ROWS, :] = shifted[:, part * ROWS : part * ROWS + wide]
        matrix = jnp.concatenate(
            [hankel[slot, :, step * LANES : step * LANES + chunk] for step in range(window // LANES)], axis=0
        )
        corr = jnp.dot(template, matrix, preferred_element_type=jnp.float32)
        term = corr * scale[s : s + 1, :] * weight
        acc = term if acc is None else acc + term

    parts = [acc[:, block * LANES : (block + 1) * LANES] for block in range(chunk // LANES)]

    @pl.when(pl.program_id(1) == 0)
    def _():
        for block, part in enumerate(parts):
            out_ref[block] = part

    @pl.when(pl.program_id(1) != 0)
    def _():
        for block, part in enumerate(parts):
            out_ref[block] += part


def station_sums(stream, temps, weights, out_len):
    stations = stream.shape[0]
    slots, lanes = weights.shape
    window = temps.shape[0] * LANES
    group = min(32, stations)
    chunk = min(1024, out_len)
    length = chunk + window
    full = stream.shape[1]
    groups = stations // group
    return pl.pallas_call(
        functools.partial(correlate_group, chunk, window),
        grid=(out_len // chunk, groups),
        in_specs=[
            pl.BlockSpec((group, full), lambda c, g: (g, 0)),
            pl.BlockSpec((window // LANES, group * slots, LANES), lambda c, g: (0, g, 0)),
            pl.BlockSpec((slots, lanes), lambda c, g: (0, 0)),
        ],
        out_specs=pl.BlockSpec((chunk // LANES, slots, LANES), lambda c, g: (c, 0, 0)),
        out_shape=jax.ShapeDtypeStruct((out_len // LANES, slots, LANES), jnp.float32),
        scratch_shapes=[
            pltpu.VMEM((group, length), jnp.float32),
            pltpu.VMEM((group, ROWS, length), jnp.bfloat16),
            pltpu.VMEM((2, LANES, length - LANES), jnp.bfloat16),
            pltpu.VMEM((group, chunk), jnp.float32),
        ],
        name="station_sums",
    )(stream, temps, weights)


def enter(peers):
    barrier = pltpu.get_barrier_semaphore()
    for peer in peers:
        pl.semaphore_signal(barrier, inc=1, device_id=peer, device_id_type=pl.DeviceIdType.MESH)
    pl.semaphore_wait(barrier, len(peers))


def collect_rows(
    count, ids_ref, records_ref, following_ref, library_ref, mask_ref, group_ref,
    stream_ref, temps_ref, weights_ref, held, tail, templates, own_sem, send_sem, recv_sem,
):
    me = lax.axis_index("tm")
    pull = pltpu.make_async_copy(library_ref, templates, own_sem.at[2])
    pull.start()
    rows, block_len = held.shape[1:]
    offset = pl.multiple_of(me * rows, rows)
    own = pltpu.make_async_copy(records_ref.at[pl.ds(offset, rows), :], held.at[me], own_sem.at[0])
    after = pltpu.make_async_copy(following_ref.at[pl.ds(offset, rows), :], tail, own_sem.at[1])
    own.start()
    after.start()
    others = [lax.rem(me + step, count) for step in range(1, count)]
    enter([{"tm": other} for other in others])
    copies = []
    for step, other in enumerate(others):
        copy = pltpu.make_async_remote_copy(
            src_ref=records_ref.at[pl.ds(pl.multiple_of(other * rows, rows), rows), :],
            dst_ref=held.at[me],
            send_sem=send_sem.at[step],
            recv_sem=recv_sem.at[step],
            device_id={"tm": other},
            device_id_type=pl.DeviceIdType.MESH,
        )
        copy.start()
        copies.append(copy)
    after.wait()
    out_len = count * block_len
    stream_ref[:, out_len:] = jnp.zeros((rows, stream_ref.shape[1] - out_len), jnp.float32)
    stream_ref[:, out_len : out_len + tail.shape[1]] = tail[...].astype(jnp.float32)

    stations = mask_ref.shape[1]
    slots, lanes = weights_ref.shape
    window = templates.shape[2]
    first = lax.axis_index("sta") * (rows * count) + offset
    turn = lax.rem(stations - first, stations)
    ids = [ids_ref[j // ids_ref.shape[1], j % ids_ref.shape[1]] for j in range(slots)]
    mask = jnp.concatenate([mask_ref[pl.ds(ids[j], 1), :] for j in range(slots)], axis=0)
    mask = mask.astype(jnp.float32)
    names = group_ref[...]
    onehot = lax.broadcasted_iota(jnp.int32, (G, stations), 0) == jnp.broadcast_to(names, (G, stations))
    counts = lax.dot_general(
        mask.astype(jnp.bfloat16),
        onehot.astype(jnp.float32).astype(jnp.bfloat16),
        (((1,), (1,)), ((), ())),
        preferred_element_type=jnp.float32,
    )
    mine = pltpu.roll(jnp.broadcast_to(names, (8, stations)), turn, 1)[:1, :lanes]
    chosen = lax.broadcasted_iota(jnp.int32, (G, lanes), 0) == jnp.broadcast_to(mine, (G, lanes))
    chosen = chosen.astype(jnp.float32).astype(jnp.bfloat16)
    high = jnp.floor(counts / 128.0) * 128.0
    low = counts - high
    per_station = jnp.dot(high.astype(jnp.bfloat16), chosen, preferred_element_type=jnp.float32) + jnp.dot(
        low.astype(jnp.bfloat16), chosen, preferred_element_type=jnp.float32
    )
    my_mask = pltpu.roll(mask, turn, 1)[:, :lanes]
    weights_ref[...] = my_mask * lax.rsqrt(jnp.float32(window * G) * jnp.maximum(per_station, 1.0))

    order = lax.broadcasted_iota(jnp.int32, (window, window), 1) ^ (ROWS - 1)
    turned = (lax.broadcasted_iota(jnp.int32, (window, window), 0) == order)
    turned = turned.astype(jnp.float32).astype(jnp.bfloat16)
    pull.wait()
    for j in range(slots):
        template = jnp.dot(templates[ids[j]], turned, preferred_element_type=jnp.float32)
        for block in range(window // LANES):
            temps_ref[block, pl.ds(j, rows, stride=slots), :] = template[:, block * LANES : (block + 1) * LANES]

    own.wait()
    for copy in copies:
        copy.wait()
    for block in range(count):
        stream_ref[:, block * block_len : (block + 1) * block_len] = held[block].astype(jnp.float32)


def collect_stream(template_ids, records, following, library, channel_mask, station_group, count):
    sta_rows, block_len = records.shape
    rows, window = library.shape[1:]
    slots = template_ids.size
    lanes = -(-rows // LANES) * LANES
    return pl.pallas_call(
        functools.partial(collect_rows, count),
        in_specs=[pl.BlockSpec(memory_space=pltpu.SMEM)]
        + [pl.BlockSpec(memory_space=pl.ANY)] * 3
        + [pl.BlockSpec(memory_space=pltpu.VMEM)] * 2,
        out_specs=[pl.BlockSpec(memory_space=pltpu.VMEM)] * 3,
        out_shape=[
            jax.ShapeDtypeStruct((rows, count * block_len + window), jnp.float32),
            jax.ShapeDtypeStruct((window // LANES, rows * slots, LANES), jnp.float32),
            jax.ShapeDtypeStruct((slots, lanes), jnp.float32),
        ],
        scratch_shapes=[
            pltpu.VMEM((count, rows, block_len), records.dtype),
            pltpu.VMEM((rows, following.shape[1]), following.dtype),
            pltpu.VMEM(library.shape, library.dtype),
            pltpu.SemaphoreType.DMA((3,)),
            pltpu.SemaphoreType.DMA((count - 1,)),
            pltpu.SemaphoreType.DMA((count - 1,)),
        ],
        compiler_params=pltpu.CompilerParams(collective_id=0, has_side_effects=True),
        name="collect_stream",
    )(template_ids, records, following, library, channel_mask, station_group.reshape(1, -1))


def reduce_blocks(parts_ref, out_ref, held, send_sem, recv_sem):
    blocks, halves = parts_ref.shape[0], parts_ref.shape[1]
    count = blocks * halves
    block, half = lax.axis_index("tm"), lax.axis_index("sta")
    me = block * halves + half
    others = []
    for step in range(1, count):
        other = lax.rem(me + step, count)
        others.append((other // halves, lax.rem(other, halves)))
    enter([{"tm": b, "sta": h} for b, h in others])
    copies = []
    for step, (b, h) in enumerate(others):
        copy = pltpu.make_async_remote_copy(
            src_ref=parts_ref.at[b, h],
            dst_ref=held.at[step],
            send_sem=send_sem.at[step],
            recv_sem=recv_sem.at[step],
            device_id={"tm": b, "sta": h},
            device_id_type=pl.DeviceIdType.MESH,
        )
        copy.start()
        copies.append(copy)
    total = parts_ref[block, half]
    for step, copy in enumerate(copies):
        copy.wait_recv()
        total = total + held[step]
    out_ref[...] = total
    for copy in copies:
        copy.wait_send()


def reduce_parts(parts):
    count = parts.shape[0] * parts.shape[1]
    return pl.pallas_call(
        reduce_blocks,
        in_specs=[pl.BlockSpec(memory_space=pltpu.VMEM)],
        out_specs=pl.BlockSpec(memory_space=pltpu.VMEM),
        out_shape=jax.ShapeDtypeStruct(parts.shape[2:], parts.dtype),
        scratch_shapes=[
            pltpu.VMEM((count - 1,) + parts.shape[2:], parts.dtype),
            pltpu.SemaphoreType.DMA((count - 1,)),
            pltpu.SemaphoreType.DMA((count - 1,)),
        ],
        compiler_params=pltpu.CompilerParams(collective_id=1, has_side_effects=True),
        name="reduce_parts",
    )(parts)


def shards(blocks, halves, records, following, library, template_ids, channel_mask, station_group):
    sta_rows, block_len = records.shape
    batches, per_batch = template_ids.shape
    stream, temps, weights = collect_stream(
        template_ids, records, following, library, channel_mask, station_group, blocks
    )
    sums = station_sums(stream, temps, weights, blocks * block_len)
    tiles = block_len // LANES
    parts = sums.reshape(blocks, tiles, halves, batches // halves * per_batch, LANES)
    parts = jnp.swapaxes(parts, 1, 2).reshape(blocks, halves, -1, LANES)
    mine = reduce_parts(parts).reshape(tiles, batches // halves, per_batch, LANES)
    return jnp.moveaxis(mine, 0, 2).reshape(batches // halves, per_batch, block_len)


def solution(mesh):
    placed = (
        P("sta", ("days", "tm")),
        P("sta", "days"),
        P(None, ("sta", "tm"), None),
        P(),
        P(),
        P(),
    )
    return jax.shard_map(
        functools.partial(shards, mesh.shape["tm"], mesh.shape["sta"]),
        mesh=mesh,
        in_specs=placed,
        out_specs=P("sta", None, ("days", "tm")),
        check_vma=False,
    )
```
